512 devices in a mesh: layer: 64 (over x_lo, z, core), rep: 8 (over y, x_hi).
Axes of the slice: x: 4 (x_hi: 2, x_lo: 2; x = x_hi * 2 + x_lo), y: 4, z: 16, core: 2. Of those that a mesh axis runs over, the one named last changes fastest.
Arguments:
- gradients: bfloat16 [8, 64, 512, 1024], P('rep', 'layer'), may hold values from -60 to 60
- inverse_out: bfloat16 [64, 512, 512], P('layer', 'rep'), may hold values from -1 to 4
- inverse_in: bfloat16 [64, 1024, 1024], P('layer', 'rep'), may hold values from -1 to 4
- cross_out: bfloat16 [64, 512, 512], P('layer', 'rep'), may hold values from -0.125 to 0.125
- cross_in: bfloat16 [64, 1024, 1024], P('layer', 'rep'), may hold values from -0.1875 to 0.1875
- momentum: float32 [64, 512, 1024], P('layer', 'rep'), may hold values from -3 to 3
Outputs:
- momentum_new: float32 [64, 512, 1024], P('layer', 'rep')
The draws below stay inside these ranges and needn't reach their ends.
All inputs are finite; a program needn't handle non-finite values.
Results may differ from the reference program's by a relative error of at most 0.003.
Values may be sent and summed in bfloat16 or wider, within the bound.
A program may use at most 64 MiB of HBM per device.

```python
import math
import jax
import jax.numpy as jnp
from jax import lax

D_OUT = 512
D_IN = 1024
LAYERS = 64
REPLICAS = 8


def factor_draw(key, count, width):
    first_key, second_key = jax.random.split(key)
    low, high, spread = (1.0, 2.0, 0.4)
    diagonal = jax.random.uniform(first_key, (count, width, 1), jnp.float32, low, high)
    off_part = jnp.clip(jax.random.normal(second_key, (count, width, width), jnp.float32), -4.0, 4.0) * (spread / math.sqrt(width))
    return off_part + diagonal * jnp.eye(width, dtype=jnp.float32)


def draw_inverse_out(key, part):
    return factor_draw(jax.random.fold_in(key, 11), LAYERS, D_OUT).astype(jnp.bfloat16)


def draw_inverse_in(key, part):
    return factor_draw(jax.random.fold_in(key, 23), LAYERS, D_IN).astype(jnp.bfloat16)


def draw_gradients(key, part):
    keys = jax.random.split(jax.random.fold_in(key, 37), 3)
    top = math.log(math.sqrt(10.0))
    base = jnp.clip(jax.random.normal(keys[0], (REPLICAS, LAYERS, D_OUT, D_IN), jnp.float32), -4.0, 4.0)
    row_scale = jnp.exp(jax.random.uniform(keys[1], (REPLICAS, LAYERS, D_OUT, 1), jnp.float32, 0.0, top))
    col_scale = jnp.exp(jax.random.uniform(keys[2], (REPLICAS, LAYERS, 1, D_IN), jnp.float32, 0.0, top))
    values = base * row_scale * col_scale
    return values.astype(jnp.bfloat16)


def block_levels(stream_key, shape, pieces, low, high):
    factor_of, own = 1.0, jax.random.fold_in(stream_key, 6)
    for axis_at, shards_of in pieces:
        steps = jnp.exp(jax.random.uniform(jax.random.fold_in(own, axis_at), (shards_of,), jnp.float32, low / len(pieces), high / len(pieces)))
        factor_of = factor_of * jnp.repeat(steps, shape[axis_at] // shards_of).reshape([-1 if axis == axis_at else 1 for axis in range(len(shape))])
    return factor_of


def normal_values(rng, extent, scale, reach, shards=(), kind=jnp.bfloat16):
    result = scale * jax.random.normal(rng, extent, jnp.float32)
    if shards:
        result = result * block_levels(rng, extent, shards, -0.22, 0.18)
    return jnp.clip(result, -reach, reach).astype(kind)


def setup_inputs(seed: int = 0) -> dict:
    arg_keys = jax.random.split(jax.random.key(seed), 7)
    return {
        "gradients": draw_gradients(jax.random.fold_in(arg_keys[6], 71), 0),
        "inverse_out": draw_inverse_out(jax.random.fold_in(arg_keys[6], 71), 0),
        "inverse_in": draw_inverse_in(jax.random.fold_in(arg_keys[6], 71), 0),
        "cross_out": normal_values(arg_keys[3], (LAYERS, D_OUT, D_OUT), (4 * D_OUT) ** -0.5, 0.125, ((0, 64), (1, 8))),
        "cross_in": normal_values(arg_keys[4], (LAYERS, D_IN, D_IN), D_IN ** -0.5, 0.1875, ((0, 64), (1, 8))),
        "momentum": normal_values(arg_keys[5], (LAYERS, D_OUT, D_IN), 0.5, 3.0, ((0, 64), (1, 8)), jnp.float32),
    }


def product(left, right):
    return jnp.dot(left.astype(jnp.float32), right.astype(jnp.float32), precision=lax.Precision.HIGHEST, preferred_element_type=jnp.float32)

def replica_step(own_block, following, carried, inv_left, inv_right, cross_left, cross_right):
    first = product(cross_left, following).astype(jnp.bfloat16)
    cross_term = product(first, cross_right)
    residual = (own_block.astype(jnp.float32) - cross_term).astype(jnp.bfloat16)
    left_applied = product(inv_left, residual).astype(jnp.bfloat16)
    precond = product(left_applied, inv_right).astype(jnp.bfloat16)
    back_product = product(cross_left.T, precond).astype(jnp.bfloat16)
    correction = product(back_product, cross_right.T).astype(jnp.bfloat16)
    update = precond.astype(jnp.float32) - carried.astype(jnp.float32)
    delta = update * lax.rsqrt(jnp.mean(update * update) + 1e-06)
    return (delta, correction)

def reference(gradients, inverse_out, inverse_in, cross_out, cross_in, momentum):
    layers_first = jnp.moveaxis(gradients, 1, 0)
    following = jnp.concatenate([layers_first[1:], jnp.zeros_like(layers_first[:1])], axis=0)

    def layer_step(carried, inputs):
        own_blocks, next_blocks, inv_left, inv_right, cross_left, cross_right = inputs
        deltas, corrections = jax.vmap(replica_step, in_axes=(0, 0, 0, None, None, None, None))(own_blocks, next_blocks, carried, inv_left, inv_right, cross_left, cross_right)
        return (corrections, lax.optimization_barrier(jnp.sum(deltas, axis=0)))
    initial = jnp.zeros((REPLICAS, D_OUT, D_IN), jnp.bfloat16)
    _, summed = lax.scan(layer_step, initial, (layers_first, following, inverse_out, inverse_in, cross_out, cross_in))
    return 0.9 * momentum + summed * (1.0 / REPLICAS)
```

```python
import functools

import jax
import jax.numpy as jnp
from jax import lax
from jax.experimental import pallas as pl
from jax.experimental.pallas import tpu as pltpu
from jax.sharding import PartitionSpec as P

MESH = pl.DeviceIdType.MESH
RING = 4
CHUNKS = 4
PER_ARRAY = 18
BF = jnp.bfloat16
F32 = jnp.float32


def dot(a, b):
    return jnp.dot(a, b, preferred_element_type=F32)


def dot_t(a, b):
    return lax.dot_general(a, b, (((1,), (1,)), ((), ())), preferred_element_type=F32)


def kernel(
    layers, reps, own_g, sh_o, sh_i, sh_x, sh_y, sh_m, out,
    f_x, f_y, f_o, f_i, xt, g_own, g_next, first, resid, left, acc, pre, back, corr, inc, ub, rb,
    sc_out, sc_in, mom, send, recv, loc,
):
    layer, rep = lax.axis_index("layer"), lax.axis_index("rep")
    y, xh = rep // 2, rep % 2
    d_out, d_in = g_own.shape
    slab = d_out // reps

    def slot_of(dy, other):
        return ((y + dy + RING) % RING) * 2 + ((1 - xh) if other else xh)

    up, down, across = (layer, slot_of(1, False)), (layer, slot_of(-1, False)), (layer, slot_of(0, True))

    local = []

    def bring(src, dst):
        c = pltpu.make_async_copy(src, dst, loc.at[len(local)])
        c.start()
        local.append(c)

    arrays = {"x": (sh_x, f_x), "y": (sh_y, f_y), "o": (sh_o, f_o), "i": (sh_i, f_i)}

    def rows_of(q, slot, part=None):
        shard, full = arrays[q]
        n = shard.shape[0]
        cols = full.shape[1]
        cut = cols * 3 // 4
        lo, size = {"a": (0, cut), "b": (cut, cols - cut), None: (0, cols)}[part]
        return n, lo, size

    def full_at(q, slot, part, half=None):
        n, lo, size = rows_of(q, slot, part)
        start, count = (0, n) if half is None else (half * (n // 2), n // 2)
        at = pl.multiple_of(slot * n + start, count)
        return arrays[q][1].at[pl.ds(at, count), pl.ds(lo, size)]

    def own_at(q, part):
        n, lo, size = rows_of(q, None, part)
        return arrays[q][0].at[pl.ds(0, n), pl.ds(lo, size)]

    for q in arrays:
        bring(arrays[q][0], full_at(q, rep, None))
    bring(own_g, g_own)
    bring(sh_m, mom)

    has_next = (layer + 1) // layers
    has_prev = (layer + layers - 1) // layers
    barrier = pltpu.get_barrier_semaphore()
    for k in range(1, reps):
        pl.semaphore_signal(barrier, inc=1, device_id=(layer, (rep + k) % reps), device_id_type=MESH)

    @pl.when(layer < layers - 1)
    def _():
        pl.semaphore_signal(barrier, inc=1, device_id=(layer + 1, rep), device_id_type=MESH)

    @pl.when(layer > 0)
    def _():
        pl.semaphore_signal(barrier, inc=1, device_id=(layer - 1, rep), device_id_type=MESH)

    pl.semaphore_wait(barrier, reps - 1 + (1 - has_next) + has_prev)

    copies = {}

    def remote(key, src, dst, device):
        i = len(copies)
        copies[key] = pltpu.make_async_remote_copy(
            src_ref=src, dst_ref=dst, send_sem=send.at[i], recv_sem=recv.at[i],
            device_id=device, device_id_type=MESH,
        )
        return copies[key]

    def put(key, src, dst, device):
        remote(key, src, dst, device).start()

    def got(*keys):
        for key in keys:
            copies[key].wait_recv()

    def begin(q):
        put((q, "ax"), own_at(q, "a"), full_at(q, rep, "a"), across)
        put((q, "bx0"), own_at(q, "b"), full_at(q, rep, "b"), across)
        put((q, "bu"), own_at(q, "b"), full_at(q, rep, "b"), up)
        put((q, "bd"), own_at(q, "b"), full_at(q, rep, "b"), down)
        put((q, "au"), own_at(q, "a"), full_at(q, rep, "a"), up)
        put((q, "ad"), own_at(q, "a"), full_at(q, rep, "a"), down)

    def pass_on(q, name, slot, part, device, half=None):
        ref = full_at(q, slot, part, half)
        put((q, name), ref, ref, device)

    def stage1(q):
        got((q, "bu"))
        pass_on(q, "bur", slot_of(-1, False), "b", up, 0)
        pass_on(q, "bx1", slot_of(-1, False), "b", across)
        got((q, "bd"))
        pass_on(q, "bdr", slot_of(1, False), "b", down, 1)
        pass_on(q, "bx2", slot_of(1, False), "b", across)
        got((q, "ax"))
        pass_on(q, "pu", slot_of(0, True), "a", up)
        pass_on(q, "pd", slot_of(0, True), "a", down)

    def stage2(q):
        got((q, "au"))
        pass_on(q, "aur", slot_of(-1, False), "a", up, 0)
        got((q, "ad"))
        pass_on(q, "adr", slot_of(1, False), "a", down, 1)
        got((q, "bur"))
        pass_on(q, "bx3", slot_of(2, False), "b", across, 0)
        got((q, "bdr"))
        pass_on(q, "bx4", slot_of(2, False), "b", across, 1)

    def stage3(q):
        got((q, "pu"))
        pass_on(q, "pur", slot_of(-1, True), "a", up, 0)
        got((q, "pd"))
        pass_on(q, "pdr", slot_of(1, True), "a", down, 1)

    def finish(q):
        for k in ("bx0", "bx1", "bx2", "aur", "adr", "bx3", "bx4", "pur", "pdr"):
            got((q, k))

    tile = d_in // CHUNKS

    def each_tile(body):
        @pl.loop(0, CHUNKS)
        def _(n):
            body(pl.ds(pl.multiple_of(n * tile, tile), tile))

    for q in "xyo":
        begin(q)
    forward = remote("g", own_g, g_next, (lax.max(layer - 1, 0), rep))

    @pl.when(layer > 0)
    def _():
        forward.start()

    stage1("x")
    stage1("y")
    begin("i")
    stage1("o")
    for q in "xyo":
        stage2(q)
    for q in "xyo":
        stage3(q)
    stage1("i")
    for c in local:
        c.wait()
    finish("x")
    xt[...] = f_x[...].T

    @pl.when(layer < layers - 1)
    def _():
        forward.wait_recv()

    @pl.when(layer == layers - 1)
    def _():
        g_next[...] = jnp.zeros_like(g_next)

    def step1(cols):
        first[:, cols] = dot(f_x[...], g_next[:, cols]).astype(BF)

    each_tile(step1)
    stage2("i")
    finish("y")

    def step2(cols):
        resid[:, cols] = (g_own[:, cols].astype(F32) - dot(first[...], f_y[:, cols])).astype(BF)

    each_tile(step2)
    stage3("i")
    finish("o")

    def step3(cols):
        left[:, cols] = dot(f_o[...], resid[:, cols]).astype(BF)

    each_tile(step3)

    depth = 2 * sh_i.shape[0]

    def part(dy):
        return pl.ds(pl.multiple_of(((y + dy + RING) % RING) * depth, depth), depth)

    got(("i", "bx0"))

    def step4_own(cols):
        acc[:, cols] = dot(left[:, part(0)], f_i[part(0), cols])

    each_tile(step4_own)
    got(("i", "bx1"), ("i", "bx2"))

    def step4_near(cols):
        acc[:, cols] += dot(left[:, part(-1)], f_i[part(-1), cols]) + dot(left[:, part(1)], f_i[part(1), cols])

    each_tile(step4_near)
    for k in ("aur", "adr", "bx3", "bx4", "pur", "pdr"):
        got(("i", k))

    def step4_far(cols):
        pre[:, cols] = (acc[:, cols] + dot(left[:, part(2)], f_i[part(2), cols])).astype(BF)

    each_tile(step4_far)

    def step5(cols):
        back[:, cols] = dot(xt[...], pre[:, cols]).astype(BF)

    each_tile(step5)

    for c in range(CHUNKS):
        cols = pl.ds(c * tile, tile)
        corr[:, cols] = dot_t(back[...], f_y[cols, :]).astype(BF)
        hop = remote(("c", c), corr.at[:, cols], inc.at[:, cols], (lax.min(layer + 1, layers - 1), rep))

        @pl.when(layer < layers - 1)
        def _(hop=hop):
            hop.start()

    @pl.when(layer == 0)
    def _():
        inc[...] = jnp.zeros_like(inc)

    total = jnp.zeros((1, 1), F32)
    for c in range(CHUNKS):
        cols = pl.ds(c * tile, tile)

        @pl.when(layer > 0)
        def _(c=c):
            copies[("c", c)].wait_recv()

        update = pre[:, cols].astype(F32) - inc[:, cols].astype(F32)
        ub[:, cols] = update.astype(BF)
        total = total + jnp.sum(update * update, keepdims=True)
        if c == CHUNKS - 1:
            scale = lax.rsqrt(total * (1.0 / (d_out * d_in)) + 1e-06)
            sc_out[...] = jnp.broadcast_to(scale, sc_out.shape)
            for k in range(1, reps):
                put(("s", k), sc_out, sc_in.at[rep], (layer, (rep + k) % reps))
        for k in range(1, reps):
            to = (rep + k) % reps
            rows = pl.ds(pl.multiple_of(to * slab, slab), slab)
            put(("u", c, k), ub.at[rows, cols], rb.at[rep, :, cols], (layer, to))

    mine = pl.ds(pl.multiple_of(rep * slab, slab), slab)
    rb[rep] = ub[mine, :]
    sc_in[rep] = sc_out[...]
    for k in range(1, reps):
        got(("s", k))
    for c in range(CHUNKS):
        for k in range(1, reps):
            got(("u", c, k))
    share = rb[0].astype(F32) * sc_in[0, 0:1, 0:1]
    for r in range(1, reps):
        share = share + rb[r].astype(F32) * sc_in[r, 0:1, 0:1]
    out[...] = 0.9 * mom[...] + share * (1.0 / reps)

    for key, c in copies.items():
        if key == "g":
            pl.when(layer > 0)(c.wait_send)
        elif key[0] == "c":
            pl.when(layer < layers - 1)(c.wait_send)
        else:
            c.wait_send()


def solution(mesh):
    layers, reps = mesh.shape["layer"], mesh.shape["rep"]

    def body(gradients, inverse_out, inverse_in, cross_out, cross_in, momentum):
        g, m = gradients[0, 0], momentum[0]
        d_out, d_in = g.shape
        n_copies = 4 * PER_ARRAY + 1 + CHUNKS + (CHUNKS + 1) * (reps - 1)
        full = pltpu.VMEM((d_out, d_in), BF)
        small, large = pltpu.VMEM((d_out, d_out), BF), pltpu.VMEM((d_in, d_in), BF)
        done = pl.pallas_call(
            functools.partial(kernel, layers, reps),
            out_shape=jax.ShapeDtypeStruct(m.shape, F32),
            in_specs=[pl.BlockSpec(memory_space=pl.ANY)] * 6,
            out_specs=pl.BlockSpec(memory_space=pltpu.VMEM),
            scratch_shapes=[
                small, large, small, large, small,
                full, full, full, full, full, pltpu.VMEM((d_out, d_in), F32), full, full, full, full, full,
                pltpu.VMEM((reps, d_out // reps, d_in), BF),
                pltpu.VMEM((8, 128), F32), pltpu.VMEM((reps, 8, 128), F32), pltpu.VMEM(m.shape, F32),
                pltpu.SemaphoreType.DMA((n_copies,)), pltpu.SemaphoreType.DMA((n_copies,)),
                pltpu.SemaphoreType.DMA((6,)),
            ],
            compiler_params=pltpu.CompilerParams(collective_id=0, has_side_effects=True),
            name="kfac_step",
        )(g, inverse_out[0], inverse_in[0], cross_out[0], cross_in[0], m)
        return done[None]

    shared = P("layer", "rep", None)
    return jax.shard_map(
        body,
        mesh=mesh,
        in_specs=(P("rep", "layer", None, None), shared, shared, shared, shared, shared),
        out_specs=shared,
        check_vma=False,
    )
```

```python
import contextlib
import functools

import jax
import jax.numpy as jnp
from jax import lax
from jax.experimental import pallas as pl
from jax.experimental.pallas import tpu as pltpu
from jax.sharding import PartitionSpec as P

MESH = pl.DeviceIdType.MESH
RING = 4
CHUNKS = 4
CUT = {"x": 4, "y": 4, "o": 4, "i": 5}
BF = jnp.bfloat16
F32 = jnp.float32


def phase(name):
    return contextlib.nullcontext()


def relay_layers(layers):
    quarter = layers // 2 // CHUNKS
    return {c: quarter * (c + 1) + 1 for c in range(CHUNKS - 1)}


def dot(a, b):
    return jnp.dot(a, b, preferred_element_type=F32)


def dot_t(a, b):
    return lax.dot_general(a, b, (((1,), (1,)), ((), ())), preferred_element_type=F32)


def kernel(
    layers, reps, own_g, sh_o, sh_i, sh_x, sh_y, out,
    f_x, f_y, f_o, f_i, xt, g_own, g_next, first, resid, left, acc, pre, back, corr, inc, ub, rb,
    sc_out, sc_in, hold, res, send, recv, loc,
):
    layer, rep = lax.axis_index("layer"), lax.axis_index("rep")
    y, xh = rep // 2, rep % 2
    d_out, d_in = g_own.shape
    slab = d_out // reps

    def slot_of(dy, other):
        return ((y + dy + RING) % RING) * 2 + ((1 - xh) if other else xh)

    up, down, across = (layer, slot_of(1, False)), (layer, slot_of(-1, False)), (layer, slot_of(0, True))

    local = []

    def bring(src, dst):
        c = pltpu.make_async_copy(src, dst, loc.at[len(local)])
        c.start()
        local.append(c)

    arrays = {"x": (sh_x, f_x), "y": (sh_y, f_y), "o": (sh_o, f_o), "i": (sh_i, f_i)}

    def rows_of(q, slot, part=None):
        shard, full = arrays[q]
        n = shard.shape[0]
        cols = full.shape[1]
        cut = cols * CUT[q] // 8
        lo, size = {"a": (0, cut), "b": (cut, cols - cut), None: (0, cols)}[part]
        return n, lo, size

    def full_at(q, slot, part, half=None):
        n, lo, size = rows_of(q, slot, part)
        start, count = (0, n) if half is None else (half * (n // 2), n // 2)
        at = pl.multiple_of(slot * n + start, count)
        return arrays[q][1].at[pl.ds(at, count), pl.ds(lo, size)]

    def own_at(q, part):
        n, lo, size = rows_of(q, None, part)
        return arrays[q][0].at[pl.ds(0, n), pl.ds(lo, size)]

    for q in arrays:
        bring(arrays[q][0], full_at(q, rep, None))
    bring(own_g, g_own)

    has_next = (layer + 1) // layers
    has_prev = (layer + layers - 1) // layers
    barrier = pltpu.get_barrier_semaphore()
    for k in range(1, reps):
        pl.semaphore_signal(barrier, inc=1, device_id=(layer, (rep + k) % reps), device_id_type=MESH)

    @pl.when(layer < layers - 1)
    def _():
        pl.semaphore_signal(barrier, inc=1, device_id=(layer + 1, rep), device_id_type=MESH)

    @pl.when(layer > 0)
    def _():
        pl.semaphore_signal(barrier, inc=1, device_id=(layer - 1, rep), device_id_type=MESH)

    half = layers // 2
    relays = relay_layers(layers)
    for at in relays.values():

        @pl.when(layer == at)
        def _():
            pl.semaphore_signal(barrier, inc=1, device_id=(half, rep), device_id_type=MESH)

    @pl.when(layer == half)
    def _():
        for k in range(1, reps):
            to = (half - 1, (rep + k) % reps)
            pl.semaphore_signal(barrier, inc=1, device_id=to, device_id_type=MESH)

    def is_layer(v):
        return (layer + layers - v) // layers - (layer + layers - v - 1) // layers

    extra = is_layer(half) * len(relays) + is_layer(half - 1) * (reps - 1)
    pl.semaphore_wait(barrier, reps - 1 + (1 - has_next) + has_prev + extra)

    tile = d_in // CHUNKS
    copies, out_at, in_at = {}, {}, {}
    last_in = ("bx0", "bx1", "bx2", "aur", "adr", "bx3", "bx4", "pur", "pdr")

    def index(table, key):
        return table.setdefault(key, len(table))

    def sender(key):
        return key[0] if key[0] in ("x", "y", "o", "i", "u", "s") else key

    def arrival(key):
        if key[0] in ("u", "s"):
            return key[0]
        if key[0] in ("x", "y", "o") and key[1] in last_in:
            return (key[0], "last")
        if key[0] == "i" and key[1] in ("bx1", "bx2"):
            return (key[0], "near")
        if key[0] == "i" and key[1] in last_in[3:]:
            return (key[0], "last")
        return key

    def remote(key, src, dst, device, arrives=None):
        c = pltpu.make_async_remote_copy(
            src_ref=src, dst_ref=dst, send_sem=send.at[index(out_at, sender(key))],
            recv_sem=recv.at[index(in_at, arrives or arrival(key))],
            device_id=device, device_id_type=MESH,
        )
        copies.setdefault(key, c)
        return c

    def await_bytes(sem, ref):
        pltpu.make_async_copy(ref, ref, sem).wait()

    def got_all(name, ref):
        await_bytes(recv.at[in_at[name]], ref)

    def sent_all(name, ref):
        await_bytes(send.at[out_at[name]], ref)

    for c in range(CHUNKS):
        index(in_at, ("c", c))

    def chunk(c):
        return pl.ds(c * tile, tile)

    def to_neighbour(name, c, src, dst, step, far, relays, near=True, beyond=True):
        end = layers - 1 if step > 0 else 0
        straight = remote((name, c), src, dst, (jnp.clip(layer + step, 0, layers - 1), rep))
        detour = remote((name, c), src, hold, (relays[c], rep), (name, "r")) if c in relays else straight
        if near:

            @pl.when((layer != end) & (layer != far))
            def _():
                straight.start()

        if beyond:

            @pl.when(layer == far)
            def _():
                detour.start()

    def relay(name, dst, step, far, relays, which):
        for c in which:
            onward = remote((name, "r"), hold, dst.at[:, chunk(c)], (far + step, rep), (name, c))

            @pl.when(layer == relays[c])
            def _(onward=onward):
                remote((name, "in"), hold, hold, (far + step, rep), (name, "r")).wait_recv()
                onward.start()
                onward.wait_send()

    def put(key, src, dst, device):
        remote(key, src, dst, device).start()

    def got(*keys):
        for key in keys:
            copies[key].wait_recv()

    def begin(q):
        put((q, "ax"), own_at(q, "a"), full_at(q, rep, "a"), across)
        put((q, "bx0"), own_at(q, "b"), full_at(q, rep, "b"), across)
        put((q, "bu"), own_at(q, "b"), full_at(q, rep, "b"), up)
        put((q, "bd"), own_at(q, "b"), full_at(q, rep, "b"), down)
        put((q, "au"), own_at(q, "a"), full_at(q, rep, "a"), up)
        put((q, "ad"), own_at(q, "a"), full_at(q, rep, "a"), down)

    def pass_on(q, name, slot, part, device, half=None):
        ref = full_at(q, slot, part, half)
        put((q, name), ref, ref, device)

    def stage1(q):
        got((q, "bu"))
        pass_on(q, "bur", slot_of(-1, False), "b", up, 0)
        pass_on(q, "bx1", slot_of(-1, False), "b", across)
        got((q, "bd"))
        pass_on(q, "bdr", slot_of(1, False), "b", down, 1)
        pass_on(q, "bx2", slot_of(1, False), "b", across)
        got((q, "ax"))
        pass_on(q, "pu", slot_of(0, True), "a", up)
        pass_on(q, "pd", slot_of(0, True), "a", down)

    def stage2(q):
        got((q, "au"))
        pass_on(q, "aur", slot_of(-1, False), "a", up, 0)
        got((q, "ad"))
        pass_on(q, "adr", slot_of(1, False), "a", down, 1)
        got((q, "bur"))
        pass_on(q, "bx3", slot_of(2, False), "b", across, 0)
        got((q, "bdr"))
        pass_on(q, "bx4", slot_of(2, False), "b", across, 1)

    def stage3(q):
        got((q, "pu"))
        pass_on(q, "pur", slot_of(-1, True), "a", up, 0)
        got((q, "pd"))
        pass_on(q, "pdr", slot_of(1, True), "a", down, 1)

    def finish(q):
        n = arrays[q][0].shape[0]
        got_all((q, "last"), arrays[q][1].at[pl.ds(0, 2 * n + n * (8 - CUT[q]) // 4), :])

    def each_tile(body):
        @pl.loop(0, CHUNKS)
        def _(n):
            body(pl.ds(pl.multiple_of(n * tile, tile), tile))

    with phase("begin"):
        for c in range(CHUNKS):
            to_neighbour("g", c, own_g.at[:, chunk(c)], g_next.at[:, chunk(c)], -1, half, relays, near=False)
        for q in "xyo":
            begin(q)
        for c in range(CHUNKS):
            to_neighbour("g", c, own_g.at[:, chunk(c)], g_next.at[:, chunk(c)], -1, half, relays, beyond=False)
    with phase("s1x"):
        stage1("x")
    with phase("s1y"):
        stage1("y")
    with phase("s1o"):
        stage1("o")
    with phase("s2x"):
        stage2("x")
    with phase("s3x"):
        stage3("x")
    with phase("s2y"):
        stage2("y")
    with phase("begin_i"):
        begin("i")
    with phase("s3y"):
        stage3("y")
    with phase("s2o"):
        stage2("o")
    with phase("s3o"):
        stage3("o")
    with phase("relay"):
        relay("g", g_next, -1, half, relays, relays)
    with phase("s1i"):
        stage1("i")
    for c in local:
        c.wait()
    with phase("fx"):
        finish("x")
    with phase("xt"):
        xt[...] = f_x[...].T

    with phase("gn"):

        @pl.when(layer < layers - 1)
        def _():
            for c in range(CHUNKS):
                copies[("g", c)].wait_recv()

        @pl.when(layer == layers - 1)
        def _():
            g_next[...] = jnp.zeros_like(g_next)

    def step1(cols):
        first[:, cols] = dot(f_x[...], g_next[:, cols]).astype(BF)

    with phase("st1"):
        each_tile(step1)
    with phase("fy"):
        finish("y")

    def step2(cols):
        resid[:, cols] = (g_own[:, cols].astype(F32) - dot(first[...], f_y[:, cols])).astype(BF)

    with phase("st2"):
        each_tile(step2)
    with phase("s2i"):
        stage2("i")
    with phase("fo"):
        finish("o")

    def step3(cols):
        left[:, cols] = dot(f_o[...], resid[:, cols]).astype(BF)

    with phase("st3"):
        each_tile(step3)
    with phase("s3i"):
        stage3("i")

    depth = 2 * sh_i.shape[0]

    def part(dy):
        return pl.ds(pl.multiple_of(((y + dy + RING) % RING) * depth, depth), depth)

    with phase("gi0"):
        got(("i", "bx0"))

    def step4_own(cols):
        acc[:, cols] = dot(left[:, part(0)], f_i[part(0), cols])

    with phase("st4a"):
        each_tile(step4_own)
    with phase("gi1"):
        n, _, rest = rows_of("i", None, "b")
        got_all(("i", "near"), f_i.at[pl.ds(0, 2 * n), pl.ds(0, rest)])

    def step4_near(cols):
        acc[:, cols] += dot(left[:, part(-1)], f_i[part(-1), cols]) + dot(left[:, part(1)], f_i[part(1), cols])

    with phase("st4b"):
        each_tile(step4_near)
    with phase("gi2"):
        got_all(("i", "last"), f_i.at[pl.ds(0, n + n * CUT["i"] // 8), :])

    def step4_far(cols):
        pre[:, cols] = (acc[:, cols] + dot(left[:, part(2)], f_i[part(2), cols])).astype(BF)

    with phase("st4c"):
        each_tile(step4_far)

    def step5(cols):
        back[:, cols] = dot(xt[...], pre[:, cols]).astype(BF)

    with phase("st5"):
        each_tile(step5)

    def rows_from(r):
        return pl.ds(pl.multiple_of(r * slab, slab), slab)

    def to_owners(name, src, dst):
        for k in range(1, reps):
            to = (rep + k) % reps
            put((name, k), src(to), dst, (layer, to))

    @pl.when(layer == half)
    def _():
        to_owners("u", lambda to: pre.at[rows_from(to), :], rb.at[rep])

    with phase("st6"):
        for c in range(CHUNKS):
            corr[:, chunk(c)] = dot_t(back[...], f_y[chunk(c), :]).astype(BF)
            src, dst = corr.at[:, chunk(c)], inc.at[:, chunk(c)]
            to_neighbour("c", c, src, dst, 1, half - 1, {}, beyond=False)

            @pl.when(layer == half - 1)
            def _(c=c):
                for k in range(reps):
                    to = (rep + k) % reps
                    there = inc.at[rows_from(rep), chunk(c)]
                    remote(("c", c), corr.at[rows_from(to), chunk(c)], there, (half, to)).start()

    @pl.when(layer == 0)
    def _():
        inc[...] = jnp.zeros_like(inc)

    for c in range(CHUNKS):
        with phase(f"inc{c}"):

            @pl.when(layer > 0)
            def _(c=c):
                copies[("c", c)].wait_recv()

        @pl.when(layer != half)
        def _(c=c):
            update = pre[:, chunk(c)].astype(F32) - inc[:, chunk(c)].astype(F32)
            ub[:, chunk(c)] = update.astype(BF)
            part = jnp.broadcast_to(jnp.sum(update * update, keepdims=True), sc_out.shape)
            total = part if c == 0 else sc_out[...] + part
            if c < CHUNKS - 1:
                sc_out[...] = total
            else:
                sc_out[...] = lax.rsqrt(total * (1.0 / (d_out * d_in)) + 1e-06)
                to_owners("s", lambda to: sc_out, sc_in.at[rep])
            to_owners("u", lambda to: ub.at[rows_from(to), chunk(c)], rb.at[rep, :, chunk(c)])

    others = reps - 1

    @pl.when(layer != half)
    def _():
        rb[rep] = ub[rows_from(rep), :]

    @pl.when(layer == half)
    def _():
        rb[rep] = pre[rows_from(rep), :]
        got_all("u", rb.at[pl.ds(0, others)])
        for r in range(reps):
            apart = rb[r].astype(F32) - inc[r * slab : (r + 1) * slab, :].astype(F32)
            acc[r * slab : (r + 1) * slab, :] = apart
            sc_out[r : r + 1, :] = jnp.broadcast_to(jnp.sum(apart * apart, keepdims=True), (1, 128))
        to_owners("s", lambda to: sc_out, sc_in.at[rep])

    with phase("sent"):
        sc_in[rep] = sc_out[...]
        for key, c in copies.items():
            if key[0] == "g" and key[1] not in ("r", "in"):
                pl.when(layer > 0)(c.wait_send)
            elif key[0] == "c":
                pl.when(layer < layers - 1)(c.wait_send)
        for q, (shard, full) in arrays.items():
            sent_all(q, full.at[pl.ds(0, others * shard.shape[0]), :])
        sent_all("s", sc_in.at[pl.ds(0, others)])
        sent_all("u", rb.at[pl.ds(0, others)])
    with phase("gots"):
        got_all("s", sc_in.at[pl.ds(0, others)])

    @pl.when(layer != half)
    def _():
        with phase("gotu"):
            got_all("u", rb.at[pl.ds(0, others)])
        with phase("sum"):
            share = rb[0].astype(F32) * sc_in[0, 0:1, 0:1]
            for r in range(1, reps):
                share = share + rb[r].astype(F32) * sc_in[r, 0:1, 0:1]
            res[...] = share * (1.0 / reps)

    @pl.when(layer == half)
    def _():
        squares = sc_in[0]
        for r in range(1, reps):
            squares = squares + sc_in[r]
        sc_out[...] = lax.rsqrt(squares * (1.0 / (d_out * d_in)) + 1e-06)
        share = acc[0:slab, :] * sc_out[0:1, 0:1]
        for r in range(1, reps):
            share = share + acc[r * slab : (r + 1) * slab, :] * sc_out[r : r + 1, 0:1]
        res[...] = share * (1.0 / reps)

    with phase("put_out"):
        c = pltpu.make_async_copy(res, out, loc.at[0])
        c.start()
        c.wait()


def solution(mesh):
    layers, reps = mesh.shape["layer"], mesh.shape["rep"]

    def body(gradients, inverse_out, inverse_in, cross_out, cross_in, momentum):
        g, m = gradients[0, 0], momentum[0]
        d_out, d_in = g.shape
        n_copies = 56
        full = pltpu.VMEM((d_out, d_in), BF)
        small, large = pltpu.VMEM((d_out, d_out), BF), pltpu.VMEM((d_in, d_in), BF)
        done = pl.pallas_call(
            functools.partial(kernel, layers, reps),
            out_shape=jax.ShapeDtypeStruct(m.shape, F32),
            in_specs=[pl.BlockSpec(memory_space=pl.ANY)] * 5,
            out_specs=pl.BlockSpec(memory_space=pl.ANY),
            scratch_shapes=[
                small, large, small, large, small,
                full, full, full, full, full, pltpu.VMEM((d_out, d_in), F32), full, full, full, full, full,
                pltpu.VMEM((reps, d_out // reps, d_in), BF),
                pltpu.VMEM((8, 128), F32), pltpu.VMEM((reps, 8, 128), F32), pltpu.VMEM((d_out, d_in // CHUNKS), BF),
                pltpu.VMEM(m.shape, F32),
                pltpu.SemaphoreType.DMA((18,)), pltpu.SemaphoreType.DMA((n_copies,)),
                pltpu.SemaphoreType.DMA((5,)),
            ],
            compiler_params=pltpu.CompilerParams(collective_id=0, has_side_effects=True),
            name="kfac_step",
        )(g, inverse_out[0], inverse_in[0], cross_out[0], cross_in[0])
        return (0.9 * m + done)[None]

    shared = P("layer", "rep", None)
    return jax.shard_map(
        body,
        mesh=mesh,
        in_specs=(P("rep", "layer", None, None), shared, shared, shared, shared, shared),
        out_specs=shared,
        check_vma=False,
    )
```

```python
import contextlib
import functools

import jax
import jax.numpy as jnp
from jax import lax
from jax.experimental import pallas as pl
from jax.experimental.pallas import tpu as pltpu
from jax.sharding import PartitionSpec as P

MESH = pl.DeviceIdType.MESH
RING = 4
CHUNKS = 4
CUT = {"x": 4, "y": 4, "o": 4, "i": 5}
BF = jnp.bfloat16
F32 = jnp.float32


def phase(name):
    return contextlib.nullcontext()


def relay_layers(layers):
    quarter = layers // 2 // CHUNKS
    return {c: quarter * (c + 1) + 1 for c in range(CHUNKS - 1)}


def dot(a, b):
    return jnp.dot(a, b, preferred_element_type=F32)


def dot_t(a, b):
    return lax.dot_general(a, b, (((1,), (1,)), ((), ())), preferred_element_type=F32)


def kernel(
    layers, reps, own_g, sh_o, sh_i, sh_x, sh_y, out,
    f_x, f_y, f_o, f_i, xt, g_own, g_next, first, resid, left, acc, pre, back, corr, inc, ub, rb,
    sc_out, sc_in, hold, send, recv, loc,
):
    layer, rep = lax.axis_index("layer"), lax.axis_index("rep")
    y, xh = rep // 2, rep % 2
    d_out, d_in = g_own.shape
    slab = d_out // reps

    def slot_of(dy, other):
        return ((y + dy + RING) % RING) * 2 + ((1 - xh) if other else xh)

    up, down, across = (layer, slot_of(1, False)), (layer, slot_of(-1, False)), (layer, slot_of(0, True))

    local = []

    def bring(src, dst):
        c = pltpu.make_async_copy(src, dst, loc.at[len(local)])
        c.start()
        local.append(c)

    arrays = {"x": (sh_x, f_x), "y": (sh_y, f_y), "o": (sh_o, f_o), "i": (sh_i, f_i)}

    def rows_of(q, slot, part=None):
        shard, full = arrays[q]
        n = shard.shape[0]
        cols = full.shape[1]
        cut = cols * CUT[q] // 8
        lo, size = {"a": (0, cut), "b": (cut, cols - cut), None: (0, cols)}[part]
        return n, lo, size

    def full_at(q, slot, part, half=None):
        n, lo, size = rows_of(q, slot, part)
        start, count = (0, n) if half is None else (half * (n // 2), n // 2)
        at = pl.multiple_of(slot * n + start, count)
        return arrays[q][1].at[pl.ds(at, count), pl.ds(lo, size)]

    def own_at(q, part):
        n, lo, size = rows_of(q, None, part)
        return full_at(q, rep, part)

    for q in arrays:
        bring(arrays[q][0], full_at(q, rep, None))
    bring(own_g, g_own)

    has_next = (layer + 1) // layers
    has_prev = (layer + layers - 1) // layers
    barrier = pltpu.get_barrier_semaphore()
    for k in range(1, reps):
        pl.semaphore_signal(barrier, inc=1, device_id=(layer, (rep + k) % reps), device_id_type=MESH)

    @pl.when(layer < layers - 1)
    def _():
        pl.semaphore_signal(barrier, inc=1, device_id=(layer + 1, rep), device_id_type=MESH)

    @pl.when(layer > 0)
    def _():
        pl.semaphore_signal(barrier, inc=1, device_id=(layer - 1, rep), device_id_type=MESH)

    half = layers // 2
    relays = relay_layers(layers)
    for at in relays.values():

        @pl.when(layer == at)
        def _():
            pl.semaphore_signal(barrier, inc=1, device_id=(half, rep), device_id_type=MESH)

    @pl.when(layer == half)
    def _():
        for k in range(1, reps):
            to = (half - 1, (rep + k) % reps)
            pl.semaphore_signal(barrier, inc=1, device_id=to, device_id_type=MESH)

    @pl.when(layer == layers - 1)
    def _():
        pl.semaphore_signal(barrier, inc=1, device_id=(half - 1, rep), device_id_type=MESH)

    def is_layer(v):
        return (layer + layers - v) // layers - (layer + layers - v - 1) // layers

    extra = is_layer(half) * len(relays) + is_layer(half - 1) * reps
    pl.semaphore_wait(barrier, reps - 1 + (1 - has_next) + has_prev + extra)

    for c in local[:4]:
        c.wait()

    tile = d_in // CHUNKS
    copies, out_at, in_at = {}, {}, {}
    last_in = ("bx0", "bx1", "bx2", "aur", "adr", "bx3", "bx4", "pur", "pdr")

    def index(table, key):
        return table.setdefault(key, len(table))

    def sender(key):
        return key[0] if key[0] in ("x", "y", "o", "i", "u", "s") else key

    def arrival(key):
        if key[0] in ("u", "s"):
            return key[0]
        if key[0] in ("x", "y", "o") and key[1] in last_in:
            return (key[0], "last")
        if key[0] == "i" and key[1] in ("bx1", "bx2"):
            return (key[0], "near")
        if key[0] == "i" and key[1] in last_in[3:]:
            return (key[0], "last")
        return key

    def remote(key, src, dst, device, arrives=None):
        c = pltpu.make_async_remote_copy(
            src_ref=src, dst_ref=dst, send_sem=send.at[index(out_at, sender(key))],
            recv_sem=recv.at[index(in_at, arrives or arrival(key))],
            device_id=device, device_id_type=MESH,
        )
        copies.setdefault(key, c)
        return c

    def await_bytes(sem, ref):
        pltpu.make_async_copy(ref, ref, sem).wait()

    def got_all(name, ref):
        await_bytes(recv.at[in_at[name]], ref)

    def sent_all(name, ref):
        await_bytes(send.at[out_at[name]], ref)

    for c in range(CHUNKS):
        index(in_at, ("c", c))

    def chunk(c):
        return pl.ds(c * tile, tile)

    def to_neighbour(name, c, src, dst, step, far, relays, near=True, beyond=True):
        end = layers - 1 if step > 0 else 0
        straight = remote((name, c), src, dst, (jnp.clip(layer + step, 0, layers - 1), rep))
        detour = remote((name, c), src, hold, (relays[c], rep), (name, "r")) if c in relays else straight
        if near:

            @pl.when((layer != end) & (layer != far))
            def _():
                straight.start()

        if beyond:

            @pl.when(layer == far)
            def _():
                detour.start()

    def relay(name, dst, step, far, relays, which):
        for c in which:
            onward = remote((name, "r"), hold, dst.at[:, chunk(c)], (far + step, rep), (name, c))

            @pl.when(layer == relays[c])
            def _(onward=onward):
                remote((name, "in"), hold, hold, (far + step, rep), (name, "r")).wait_recv()
                onward.start()
                onward.wait_send()

    def put(key, src, dst, device):
        remote(key, src, dst, device).start()

    def got(*keys):
        for key in keys:
            copies[key].wait_recv()

    def begin(q):
        put((q, "ax"), own_at(q, "a"), full_at(q, rep, "a"), across)
        put((q, "bx0"), own_at(q, "b"), full_at(q, rep, "b"), across)
        put((q, "bu"), own_at(q, "b"), full_at(q, rep, "b"), up)
        put((q, "bd"), own_at(q, "b"), full_at(q, rep, "b"), down)
        put((q, "au"), own_at(q, "a"), full_at(q, rep, "a"), up)
        put((q, "ad"), own_at(q, "a"), full_at(q, rep, "a"), down)

    def pass_on(q, name, slot, part, device, half=None):
        ref = full_at(q, slot, part, half)
        put((q, name), ref, ref, device)

    def stage1(q):
        got((q, "bu"))
        pass_on(q, "bur", slot_of(-1, False), "b", up, 0)
        pass_on(q, "bx1", slot_of(-1, False), "b", across)
        got((q, "bd"))
        pass_on(q, "bdr", slot_of(1, False), "b", down, 1)
        pass_on(q, "bx2", slot_of(1, False), "b", across)
        got((q, "ax"))
        pass_on(q, "pu", slot_of(0, True), "a", up)
        pass_on(q, "pd", slot_of(0, True), "a", down)

    def stage2(q):
        got((q, "au"))
        pass_on(q, "aur", slot_of(-1, False), "a", up, 0)
        got((q, "ad"))
        pass_on(q, "adr", slot_of(1, False), "a", down, 1)
        got((q, "bur"))
        pass_on(q, "bx3", slot_of(2, False), "b", across, 0)
        got((q, "bdr"))
        pass_on(q, "bx4", slot_of(2, False), "b", across, 1)

    def stage3(q):
        got((q, "pu"))
        pass_on(q, "pur", slot_of(-1, True), "a", up, 0)
        got((q, "pd"))
        pass_on(q, "pdr", slot_of(1, True), "a", down, 1)

    def finish(q):
        n = arrays[q][0].shape[0]
        got_all((q, "last"), arrays[q][1].at[pl.ds(0, 2 * n + n * (8 - CUT[q]) // 4), :])

    def each_tile(body):
        @pl.loop(0, CHUNKS)
        def _(n):
            body(pl.ds(pl.multiple_of(n * tile, tile), tile))

    with phase("begin"):
        for c in range(CHUNKS):
            to_neighbour("g", c, own_g.at[:, chunk(c)], g_next.at[:, chunk(c)], -1, half, relays, near=False)
        for q in "xyo":
            begin(q)
        for c in range(CHUNKS):
            to_neighbour("g", c, own_g.at[:, chunk(c)], g_next.at[:, chunk(c)], -1, half, relays, beyond=False)
    with phase("s1x"):
        stage1("x")
    with phase("s1y"):
        stage1("y")
    with phase("s1o"):
        stage1("o")
    with phase("s2x"):
        stage2("x")
    with phase("s3x"):
        stage3("x")
    with phase("s2y"):
        stage2("y")
    with phase("begin_i"):
        begin("i")
    with phase("s3y"):
        stage3("y")
    with phase("s2o"):
        stage2("o")
    with phase("s3o"):
        stage3("o")
    with phase("relay"):
        relay("g", g_next, -1, half, relays, relays)
    with phase("s1i"):
        stage1("i")
    for c in local[4:]:
        c.wait()
    with phase("fx"):
        finish("x")
    with phase("xt"):
        xt[...] = f_x[...].T

    with phase("gn"):

        @pl.when(layer < layers - 1)
        def _():
            for c in range(CHUNKS):
                copies[("g", c)].wait_recv()

        @pl.when(layer == layers - 1)
        def _():
            g_next[...] = jnp.zeros_like(g_next)

    def step1(cols):
        first[:, cols] = dot(f_x[...], g_next[:, cols]).astype(BF)

    with phase("st1"):
        each_tile(step1)
    with phase("fy"):
        finish("y")

    def step2(cols):
        resid[:, cols] = (g_own[:, cols].astype(F32) - dot(first[...], f_y[:, cols])).astype(BF)

    with phase("st2"):
        each_tile(step2)
    with phase("s2i"):
        stage2("i")
    with phase("fo"):
        finish("o")

    def step3(cols):
        left[:, cols] = dot(f_o[...], resid[:, cols]).astype(BF)

    with phase("st3"):
        each_tile(step3)
    with phase("s3i"):
        stage3("i")

    depth = 2 * sh_i.shape[0]

    def part(dy):
        return pl.ds(pl.multiple_of(((y + dy + RING) % RING) * depth, depth), depth)

    with phase("gi0"):
        got(("i", "bx0"))

    def step4_own(cols):
        acc[:, cols] = dot(left[:, part(0)], f_i[part(0), cols])

    with phase("st4a"):
        each_tile(step4_own)
    with phase("gi1"):
        n, _, rest = rows_of("i", None, "b")
        got_all(("i", "near"), f_i.at[pl.ds(0, 2 * n), pl.ds(0, rest)])

    def step4_near(cols):
        acc[:, cols] += dot(left[:, part(-1)], f_i[part(-1), cols]) + dot(left[:, part(1)], f_i[part(1), cols])

    with phase("st4b"):
        each_tile(step4_near)
    with phase("gi2"):
        got_all(("i", "last"), f_i.at[pl.ds(0, n + n * CUT["i"] // 8), :])

    def step4_far(cols):
        pre[:, cols] = (acc[:, cols] + dot(left[:, part(2)], f_i[part(2), cols])).astype(BF)

    with phase("st4c"):
        each_tile(step4_far)

    def step5(cols):
        back[:, cols] = dot(xt[...], pre[:, cols]).astype(BF)

    with phase("st5"):
        each_tile(step5)

    def rows_from(r):
        return pl.ds(pl.multiple_of(r * slab, slab), slab)

    def to_owners(name, src, dst):
        for k in range(1, reps):
            to = (rep + k) % reps
            put((name, k), src(to), dst, (layer, to))

    @pl.when(layer == half)
    def _():
        to_owners("u", lambda to: pre.at[rows_from(to), :], rb.at[rep])

    def to_far_owners(key, src, c):
        for k in range(reps):
            to = (rep + k) % reps
            remote(key, src(to), inc.at[rows_from(rep), chunk(c)], (half, to), ("c", c)).start()

    with phase("st6"):
        for c in range(CHUNKS):
            corr[:, chunk(c)] = dot_t(back[...], f_y[chunk(c), :]).astype(BF)
            src, dst = corr.at[:, chunk(c)], inc.at[:, chunk(c)]
            to_neighbour("c", c, src, dst, 1, half - 1, {}, beyond=False)

            @pl.when(layer == half - 1)
            def _(c=c):
                if c == 0:
                    remote(("c", 0), corr.at[:, chunk(0)], hold, (layers - 1, rep), ("c", "r")).start()
                else:
                    to_far_owners(("c", c), lambda to: corr.at[rows_from(to), chunk(c)], c)

    @pl.when(layer == 0)
    def _():
        inc[...] = jnp.zeros_like(inc)

    with phase("relay_c"):

        @pl.when(layer == layers - 1)
        def _():
            got_all(("c", "r"), hold)
            to_far_owners(("c", "r"), lambda to: hold.at[rows_from(to), :], 0)

    for c in range(CHUNKS):
        with phase(f"inc{c}"):

            @pl.when((layer > 0) & (layer != half))
            def _(c=c):
                copies[("c", c)].wait_recv()

        @pl.when(layer != half)
        def _(c=c):
            update = pre[:, chunk(c)].astype(F32) - inc[:, chunk(c)].astype(F32)
            ub[:, chunk(c)] = update.astype(BF)
            part = jnp.broadcast_to(jnp.sum(update * update, keepdims=True), sc_out.shape)
            total = part if c == 0 else sc_out[...] + part
            if c < CHUNKS - 1:
                sc_out[...] = total
            else:
                sc_out[...] = lax.rsqrt(total * (1.0 / (d_out * d_in)) + 1e-06)
                to_owners("s", lambda to: sc_out, sc_in.at[rep])
            to_owners("u", lambda to: ub.at[rows_from(to), chunk(c)], rb.at[rep, :, chunk(c)])

    others = reps - 1

    @pl.when(layer != half)
    def _():
        rb[rep] = ub[rows_from(rep), :]

    @pl.when(layer == half)
    def _():
        rb[rep] = pre[rows_from(rep), :]
        got_all("u", rb.at[pl.ds(0, others)])
        order = [*range(1, CHUNKS), 0]
        for c in order:
            with phase(f"far{c}"):
                copies[("c", c)].wait_recv()
            for r in range(reps):
                apart = rb[r, :, chunk(c)].astype(F32) - inc[r * slab : (r + 1) * slab, chunk(c)].astype(F32)
                acc[r * slab : (r + 1) * slab, chunk(c)] = apart
                squares = jnp.broadcast_to(jnp.sum(apart * apart, keepdims=True), (1, 128))
                sc_out[r : r + 1, :] = squares if c == order[0] else sc_out[r : r + 1, :] + squares
        to_owners("s", lambda to: sc_out, sc_in.at[rep])

    with phase("sent"):
        sc_in[rep] = sc_out[...]
        for key, c in copies.items():
            if key[0] == "g" and key[1] not in ("r", "in"):
                pl.when(layer > 0)(c.wait_send)
            elif key[0] == "c" and key[1] != "r":
                pl.when(layer < layers - 1)(c.wait_send)
        for q, (shard, full) in arrays.items():
            sent_all(q, full.at[pl.ds(0, others * shard.shape[0]), :])
        sent_all("s", sc_in.at[pl.ds(0, others)])

        @pl.when(layer == layers - 1)
        def _():
            sent_all(("c", "r"), hold)

        sent_all("u", rb.at[pl.ds(0, others)])
    with phase("gots"):
        got_all("s", sc_in.at[pl.ds(0, others)])

    @pl.when(layer != half)
    def _():
        with phase("gotu"):
            got_all("u", rb.at[pl.ds(0, others)])
        with phase("sum"):
            share = rb[0].astype(F32) * sc_in[0, 0:1, 0:1]
            for r in range(1, reps):
                share = share + rb[r].astype(F32) * sc_in[r, 0:1, 0:1]
            out[...] = share * (1.0 / reps)

    @pl.when(layer == half)
    def _():
        squares = sc_in[0]
        for r in range(1, reps):
            squares = squares + sc_in[r]
        sc_out[...] = lax.rsqrt(squares * (1.0 / (d_out * d_in)) + 1e-06)
        share = acc[0:slab, :] * sc_out[0:1, 0:1]
        for r in range(1, reps):
            share = share + acc[r * slab : (r + 1) * slab, :] * sc_out[r : r + 1, 0:1]
        out[...] = share * (1.0 / reps)


def solution(mesh):
    layers, reps = mesh.shape["layer"], mesh.shape["rep"]

    def body(gradients, inverse_out, inverse_in, cross_out, cross_in, momentum):
        g, m = gradients[0, 0], momentum[0]
        d_out, d_in = g.shape
        n_copies = 56
        full = pltpu.VMEM((d_out, d_in), BF)
        small, large = pltpu.VMEM((d_out, d_out), BF), pltpu.VMEM((d_in, d_in), BF)
        done = pl.pallas_call(
            functools.partial(kernel, layers, reps),
            out_shape=pltpu.VMEM(m.shape, F32),
            in_specs=[pl.BlockSpec(memory_space=pl.ANY)] * 5,
            out_specs=pl.BlockSpec(memory_space=pltpu.VMEM),
            scratch_shapes=[
                small, large, small, large, small,
                full, full, full, full, full, pltpu.VMEM((d_out, d_in), F32), full, full, full, full, full,
                pltpu.VMEM((reps, d_out // reps, d_in), BF),
                pltpu.VMEM((8, 128), F32), pltpu.VMEM((reps, 8, 128), F32), pltpu.VMEM((d_out, d_in // CHUNKS), BF),
                pltpu.SemaphoreType.DMA((18,)), pltpu.SemaphoreType.DMA((n_copies,)),
                pltpu.SemaphoreType.DMA((5,)),
            ],
            compiler_params=pltpu.CompilerParams(collective_id=0, has_side_effects=True),
            name="kfac_step",
        )(g, inverse_out[0], inverse_in[0], cross_out[0], cross_in[0])
        return (0.9 * m + done)[None]

    shared = P("layer", "rep", None)
    return jax.shard_map(
        body,
        mesh=mesh,
        in_specs=(P("rep", "layer", None, None), shared, shared, shared, shared, shared),
        out_specs=shared,
        check_vma=False,
    )
```

```python
import contextlib
import functools

import jax
import jax.numpy as jnp
from jax import lax
from jax.experimental import pallas as pl
from jax.experimental.pallas import tpu as pltpu
from jax.sharding import PartitionSpec as P

MESH = pl.DeviceIdType.MESH
RING = 4
CHUNKS = 4
CUT = {"x": 4, "y": 4, "o": 4, "i": 5}
BF = jnp.bfloat16
F32 = jnp.float32


def phase(name):
    return contextlib.nullcontext()


def relay_layers(layers):
    quarter = layers // 2 // CHUNKS
    return {c: quarter * (c + 1) + 1 for c in range(CHUNKS - 1)}


def dot(a, b):
    return jnp.dot(a, b, preferred_element_type=F32)


def dot_t(a, b):
    return lax.dot_general(a, b, (((1,), (1,)), ((), ())), preferred_element_type=F32)


def kernel(
    layers, reps, own_g, sh_o, sh_i, sh_x, sh_y, out,
    f_x, f_y, f_o, f_i, xt, g_own, g_next, first, resid, left, acc, pre, back, corr, inc, ub, rb,
    sc_out, sc_in, hold, send, recv, loc, turn,
):
    layer, rep = lax.axis_index("layer"), lax.axis_index("rep")
    y, xh = rep // 2, rep % 2
    d_out, d_in = g_own.shape
    slab = d_out // reps

    def slot_of(dy, other):
        return ((y + dy + RING) % RING) * 2 + ((1 - xh) if other else xh)

    up, down, across = (layer, slot_of(1, False)), (layer, slot_of(-1, False)), (layer, slot_of(0, True))

    local = []

    def bring(src, dst):
        c = pltpu.make_async_copy(src, dst, loc.at[len(local)])
        c.start()
        local.append(c)

    arrays = {"x": (sh_x, f_x), "y": (sh_y, f_y), "o": (sh_o, f_o), "i": (sh_i, f_i)}

    def rows_of(q, slot, part=None):
        shard, full = arrays[q]
        n = shard.shape[0]
        cols = full.shape[1]
        cut = cols * CUT[q] // 8
        lo, size = {"a": (0, cut), "b": (cut, cols - cut), None: (0, cols)}[part]
        return n, lo, size

    def full_at(q, slot, part, half=None):
        n, lo, size = rows_of(q, slot, part)
        start, count = (0, n) if half is None else (half * (n // 2), n // 2)
        at = pl.multiple_of(slot * n + start, count)
        return arrays[q][1].at[pl.ds(at, count), pl.ds(lo, size)]

    def own_at(q, part):
        n, lo, size = rows_of(q, None, part)
        return full_at(q, rep, part)

    for q in arrays:
        bring(arrays[q][0], full_at(q, rep, None))
    bring(own_g, g_own)

    has_next = (layer + 1) // layers
    has_prev = (layer + layers - 1) // layers
    barrier = pltpu.get_barrier_semaphore()
    for k in range(1, reps):
        pl.semaphore_signal(barrier, inc=1, device_id=(layer, (rep + k) % reps), device_id_type=MESH)

    @pl.when(layer < layers - 1)
    def _():
        pl.semaphore_signal(barrier, inc=1, device_id=(layer + 1, rep), device_id_type=MESH)

    @pl.when(layer > 0)
    def _():
        pl.semaphore_signal(barrier, inc=1, device_id=(layer - 1, rep), device_id_type=MESH)

    half = layers // 2
    relays = relay_layers(layers)
    for at in relays.values():

        @pl.when(layer == at)
        def _():
            pl.semaphore_signal(barrier, inc=1, device_id=(half, rep), device_id_type=MESH)

    @pl.when(layer == half)
    def _():
        for k in range(1, reps):
            to = (half - 1, (rep + k) % reps)
            pl.semaphore_signal(barrier, inc=1, device_id=to, device_id_type=MESH)

    @pl.when(layer == layers - 1)
    def _():
        pl.semaphore_signal(barrier, inc=1, device_id=(half - 1, rep), device_id_type=MESH)

    def is_layer(v):
        return (layer + layers - v) // layers - (layer + layers - v - 1) // layers

    extra = is_layer(half) * len(relays) + is_layer(half - 1) * reps
    pl.semaphore_wait(barrier, reps - 1 + (1 - has_next) + has_prev + extra)

    for c in local[:4]:
        c.wait()

    tile = d_in // CHUNKS
    copies, out_at, in_at = {}, {}, {}
    last_in = ("bx0", "bx1", "bx2", "aur", "adr", "bx3", "bx4", "pur", "pdr")

    def index(table, key):
        return table.setdefault(key, len(table))

    def sender(key):
        return key[0] if key[0] in ("x", "y", "o", "i", "u", "s") else key

    def arrival(key):
        if key[0] in ("u", "s"):
            return key[0]
        if key[0] in ("x", "y", "o") and key[1] in last_in:
            return (key[0], "last")
        if key[0] == "i" and key[1] in ("bx1", "bx2"):
            return (key[0], "near")
        if key[0] == "i" and key[1] in last_in[3:]:
            return (key[0], "last")
        return key

    def remote(key, src, dst, device, arrives=None):
        c = pltpu.make_async_remote_copy(
            src_ref=src, dst_ref=dst, send_sem=send.at[index(out_at, sender(key))],
            recv_sem=recv.at[index(in_at, arrives or arrival(key))],
            device_id=device, device_id_type=MESH,
        )
        copies.setdefault(key, c)
        return c

    def await_bytes(sem, ref):
        pltpu.make_async_copy(ref, ref, sem).wait()

    def got_all(name, ref):
        await_bytes(recv.at[in_at[name]], ref)

    def sent_all(name, ref):
        await_bytes(send.at[out_at[name]], ref)

    for c in range(CHUNKS):
        index(in_at, ("c", c))

    def chunk(c):
        return pl.ds(c * tile, tile)

    def to_neighbour(name, c, src, dst, step, far, relays, near=True, beyond=True):
        end = layers - 1 if step > 0 else 0
        straight = remote((name, c), src, dst, (jnp.clip(layer + step, 0, layers - 1), rep))
        detour = remote((name, c), src, hold, (relays[c], rep), (name, "r")) if c in relays else straight
        if near:

            @pl.when((layer != end) & (layer != far))
            def _():
                straight.start()

        if beyond:

            @pl.when(layer == far)
            def _():
                detour.start()

    def relay(name, dst, step, far, relays, which):
        for c in which:
            onward = remote((name, "r"), hold, dst.at[:, chunk(c)], (far + step, rep), (name, c))

            @pl.when(layer == relays[c])
            def _(onward=onward):
                remote((name, "in"), hold, hold, (far + step, rep), (name, "r")).wait_recv()
                onward.start()
                onward.wait_send()

    def put(key, src, dst, device):
        remote(key, src, dst, device).start()

    def got(*keys):
        for key in keys:
            copies[key].wait_recv()

    def begin(q):
        put((q, "ax"), own_at(q, "a"), full_at(q, rep, "a"), across)
        put((q, "bx0"), own_at(q, "b"), full_at(q, rep, "b"), across)
        put((q, "bu"), own_at(q, "b"), full_at(q, rep, "b"), up)
        put((q, "bd"), own_at(q, "b"), full_at(q, rep, "b"), down)
        put((q, "au"), own_at(q, "a"), full_at(q, rep, "a"), up)
        put((q, "ad"), own_at(q, "a"), full_at(q, rep, "a"), down)

    def pass_on(q, name, slot, part, device, half=None):
        ref = full_at(q, slot, part, half)
        put((q, name), ref, ref, device)

    def stage1(q):
        got((q, "bu"))
        pass_on(q, "bur", slot_of(-1, False), "b", up, 0)
        pass_on(q, "bx1", slot_of(-1, False), "b", across)
        got((q, "bd"))
        pass_on(q, "bdr", slot_of(1, False), "b", down, 1)
        pass_on(q, "bx2", slot_of(1, False), "b", across)
        got((q, "ax"))
        pass_on(q, "pu", slot_of(0, True), "a", up)
        pass_on(q, "pd", slot_of(0, True), "a", down)

    def stage2(q):
        got((q, "au"))
        pass_on(q, "aur", slot_of(-1, False), "a", up, 0)
        got((q, "ad"))
        pass_on(q, "adr", slot_of(1, False), "a", down, 1)
        got((q, "bur"))
        pass_on(q, "bx3", slot_of(2, False), "b", across, 0)
        got((q, "bdr"))
        pass_on(q, "bx4", slot_of(2, False), "b", across, 1)

    def stage3(q):
        got((q, "pu"))
        pass_on(q, "pur", slot_of(-1, True), "a", up, 0)
        got((q, "pd"))
        pass_on(q, "pdr", slot_of(1, True), "a", down, 1)

    def finish(q):
        n = arrays[q][0].shape[0]
        got_all((q, "last"), arrays[q][1].at[pl.ds(0, 2 * n + n * (8 - CUT[q]) // 4), :])

    def each_tile(body):
        @pl.loop(0, CHUNKS)
        def _(n):
            body(pl.ds(pl.multiple_of(n * tile, tile), tile))

    with phase("begin"):
        for c in range(CHUNKS):
            to_neighbour("g", c, own_g.at[:, chunk(c)], g_next.at[:, chunk(c)], -1, half, relays, near=False)
        for q in "xyo":
            begin(q)
        for c in range(CHUNKS):
            to_neighbour("g", c, own_g.at[:, chunk(c)], g_next.at[:, chunk(c)], -1, half, relays, beyond=False)
    with phase("s1x"):
        stage1("x")
    with phase("s1y"):
        stage1("y")
    with phase("s1o"):
        stage1("o")
    with phase("s2x"):
        stage2("x")
    with phase("s3x"):
        stage3("x")
    with phase("s2y"):
        stage2("y")
    with phase("begin_i"):
        begin("i")
    with phase("s3y"):
        stage3("y")
    with phase("s2o"):
        stage2("o")
    with phase("s3o"):
        stage3("o")
    with phase("relay"):
        relay("g", g_next, -1, half, relays, relays)
    with phase("s1i"):
        stage1("i")
    for c in local[4:]:
        c.wait()
    with phase("fx"):
        finish("x")
    with phase("xt"):
        xt[...] = f_x[...].T

    with phase("gn"):

        @pl.when(layer < layers - 1)
        def _():
            for c in range(CHUNKS):
                copies[("g", c)].wait_recv()

        @pl.when(layer == layers - 1)
        def _():
            g_next[...] = jnp.zeros_like(g_next)

    def step1(cols):
        first[:, cols] = dot(f_x[...], g_next[:, cols]).astype(BF)

    with phase("st1"):
        each_tile(step1)
    with phase("fy"):
        finish("y")

    def step2(cols):
        resid[:, cols] = (g_own[:, cols].astype(F32) - dot(first[...], f_y[:, cols])).astype(BF)

    with phase("st2"):
        each_tile(step2)
    with phase("s2i"):
        stage2("i")
    with phase("fo"):
        finish("o")

    def step3(cols):
        left[:, cols] = dot(f_o[...], resid[:, cols]).astype(BF)

    with phase("st3"):
        each_tile(step3)
    with phase("s3i"):
        stage3("i")

    depth = 2 * sh_i.shape[0]

    def part(dy):
        return pl.ds(pl.multiple_of(((y + dy + RING) % RING) * depth, depth), depth)

    with phase("gi0"):
        got(("i", "bx0"))

    def step4_own(cols):
        acc[:, cols] = dot(left[:, part(0)], f_i[part(0), cols])

    with phase("st4a"):
        each_tile(step4_own)
    with phase("gi1"):
        n, _, rest = rows_of("i", None, "b")
        got_all(("i", "near"), f_i.at[pl.ds(0, 2 * n), pl.ds(0, rest)])

    def step4_near(cols):
        acc[:, cols] += dot(left[:, part(-1)], f_i[part(-1), cols]) + dot(left[:, part(1)], f_i[part(1), cols])

    with phase("st4b"):
        each_tile(step4_near)
    with phase("gi2"):
        got_all(("i", "last"), f_i.at[pl.ds(0, n + n * CUT["i"] // 8), :])

    def step4_far(cols):
        pre[:, cols] = (acc[:, cols] + dot(left[:, part(2)], f_i[part(2), cols])).astype(BF)

    with phase("st4c"):
        each_tile(step4_far)

    def step5(cols):
        back[:, cols] = dot(xt[...], pre[:, cols]).astype(BF)

    with phase("st5"):
        each_tile(step5)

    def rows_from(r):
        return pl.ds(pl.multiple_of(r * slab, slab), slab)

    def to_owners(name, src, dst):
        for k in range(1, reps):
            to = (rep + k) % reps
            put((name, k), src(to), dst, (layer, to))

    @pl.when(layer == half)
    def _():
        to_owners("u", lambda to: pre.at[rows_from(to), :], rb.at[rep])

    def to_far_owners(key, src, c):
        for k in range(reps):
            to = (rep + k) % reps
            remote(key, src(to), inc.at[rows_from(rep), chunk(c)], (half, to), ("c", c)).start()

    with phase("st6"):
        for c in range(CHUNKS):
            corr[:, chunk(c)] = dot_t(back[...], f_y[chunk(c), :]).astype(BF)
            src, dst = corr.at[:, chunk(c)], inc.at[:, chunk(c)]
            to_neighbour("c", c, src, dst, 1, half - 1, {}, beyond=False)

            @pl.when(layer == half - 1)
            def _(c=c):
                if c == 0:
                    remote(("c", 0), corr.at[:, chunk(0)], hold, (layers - 1, rep), ("c", "r")).start()
                else:
                    to_far_owners(("c", c), lambda to: corr.at[rows_from(to), chunk(c)], c)

    @pl.when(layer == 0)
    def _():
        inc[...] = jnp.zeros_like(inc)

    with phase("relay_c"):

        @pl.when(layer == layers - 1)
        def _():
            got_all(("c", "r"), hold)
            to_far_owners(("c", "r"), lambda to: hold.at[rows_from(to), :], 0)

    with phase("turn"):

        @pl.when(layer == half + 1)
        def _():
            pl.semaphore_wait(turn, 1)

    for c in range(CHUNKS):
        with phase(f"inc{c}"):

            @pl.when((layer > 0) & (layer != half))
            def _(c=c):
                copies[("c", c)].wait_recv()

        @pl.when(layer != half)
        def _(c=c):
            update = pre[:, chunk(c)].astype(F32) - inc[:, chunk(c)].astype(F32)
            ub[:, chunk(c)] = update.astype(BF)
            part = jnp.broadcast_to(jnp.sum(update * update, keepdims=True), sc_out.shape)
            total = part if c == 0 else sc_out[...] + part
            if c < CHUNKS - 1:
                sc_out[...] = total
            else:
                sc_out[...] = lax.rsqrt(total * (1.0 / (d_out * d_in)) + 1e-06)
                to_owners("s", lambda to: sc_out, sc_in.at[rep])
            to_owners("u", lambda to: ub.at[rows_from(to), chunk(c)], rb.at[rep, :, chunk(c)])

    others = reps - 1

    @pl.when(layer != half)
    def _():
        rb[rep] = ub[rows_from(rep), :]

    @pl.when(layer == half)
    def _():
        rb[rep] = pre[rows_from(rep), :]
        got_all("u", rb.at[pl.ds(0, others)])
        pl.semaphore_signal(turn, inc=1, device_id=(half + 1, rep), device_id_type=MESH)
        order = [*range(1, CHUNKS), 0]
        for c in order:
            with phase(f"far{c}"):
                copies[("c", c)].wait_recv()
            for r in range(reps):
                apart = rb[r, :, chunk(c)].astype(F32) - inc[r * slab : (r + 1) * slab, chunk(c)].astype(F32)
                acc[r * slab : (r + 1) * slab, chunk(c)] = apart
                squares = jnp.broadcast_to(jnp.sum(apart * apart, keepdims=True), (1, 128))
                sc_out[r : r + 1, :] = squares if c == order[0] else sc_out[r : r + 1, :] + squares
        to_owners("s", lambda to: sc_out, sc_in.at[rep])

    with phase("sent"):
        sc_in[rep] = sc_out[...]
        for key, c in copies.items():
            if key[0] == "g" and key[1] not in ("r", "in"):
                pl.when(layer > 0)(c.wait_send)
            elif key[0] == "c" and key[1] != "r":
                pl.when(layer < layers - 1)(c.wait_send)
        for q, (shard, full) in arrays.items():
            sent_all(q, full.at[pl.ds(0, others * shard.shape[0]), :])
        sent_all("s", sc_in.at[pl.ds(0, others)])

        @pl.when(layer == layers - 1)
        def _():
            sent_all(("c", "r"), hold)

        sent_all("u", rb.at[pl.ds(0, others)])
    with phase("gots"):
        got_all("s", sc_in.at[pl.ds(0, others)])

    @pl.when(layer != half)
    def _():
        with phase("gotu"):
            got_all("u", rb.at[pl.ds(0, others)])
        with phase("sum"):
            share = rb[0].astype(F32) * sc_in[0, 0:1, 0:1]
            for r in range(1, reps):
                share = share + rb[r].astype(F32) * sc_in[r, 0:1, 0:1]
            out[...] = share * (1.0 / reps)

    @pl.when(layer == half)
    def _():
        squares = sc_in[0]
        for r in range(1, reps):
            squares = squares + sc_in[r]
        sc_out[...] = lax.rsqrt(squares * (1.0 / (d_out * d_in)) + 1e-06)
        share = acc[0:slab, :] * sc_out[0:1, 0:1]
        for r in range(1, reps):
            share = share + acc[r * slab : (r + 1) * slab, :] * sc_out[r : r + 1, 0:1]
        out[...] = share * (1.0 / reps)


def solution(mesh):
    layers, reps = mesh.shape["layer"], mesh.shape["rep"]

    def body(gradients, inverse_out, inverse_in, cross_out, cross_in, momentum):
        g, m = gradients[0, 0], momentum[0]
        d_out, d_in = g.shape
        n_copies = 56
        full = pltpu.VMEM((d_out, d_in), BF)
        small, large = pltpu.VMEM((d_out, d_out), BF), pltpu.VMEM((d_in, d_in), BF)
        done = pl.pallas_call(
            functools.partial(kernel, layers, reps),
            out_shape=pltpu.VMEM(m.shape, F32),
            in_specs=[pl.BlockSpec(memory_space=pl.ANY)] * 5,
            out_specs=pl.BlockSpec(memory_space=pltpu.VMEM),
            scratch_shapes=[
                small, large, small, large, small,
                full, full, full, full, full, pltpu.VMEM((d_out, d_in), F32), full, full, full, full, full,
                pltpu.VMEM((reps, d_out // reps, d_in), BF),
                pltpu.VMEM((8, 128), F32), pltpu.VMEM((reps, 8, 128), F32), pltpu.VMEM((d_out, d_in // CHUNKS), BF),
                pltpu.SemaphoreType.DMA((18,)), pltpu.SemaphoreType.DMA((n_copies,)),
                pltpu.SemaphoreType.DMA((5,)), pltpu.SemaphoreType.REGULAR,
            ],
            compiler_params=pltpu.CompilerParams(collective_id=0, has_side_effects=True),
            name="kfac_step",
        )(g, inverse_out[0], inverse_in[0], cross_out[0], cross_in[0])
        return (0.9 * m + done)[None]

    shared = P("layer", "rep", None)
    return jax.shard_map(
        body,
        mesh=mesh,
        in_specs=(P("rep", "layer", None, None), shared, shared, shared, shared, shared),
        out_specs=shared,
        check_vma=False,
    )
```
